32 devices in a mesh: job: 2 (over y), chain: 4 (over z), pair: 2 (over x), pno: 2 (over core).
Axes of the slice: x: 2, y: 2, z: 4, core: 2. Of those that a mesh axis runs over, the one named last changes fastest.
Arguments:
- amplitudes: bfloat16 [96, 128, 128], P(('job', 'chain', 'pair'), 'pno'), parts along dimension 0, may hold values from -4 to 4
- integrals: bfloat16 [96, 128, 128], P(('job', 'chain', 'pair'), 'pno'), parts along dimension 0, may hold values from -6 to 6
- intersections: bfloat16 [96, 32, 128, 128], P(('job', 'chain', 'pair')), parts along dimension 0, may hold values from -0.5 to 0.5
- coupling: float32 [96, 32], P(('job', 'chain', 'pair')), parts along dimension 0, may hold values from -4 to 4
- pno_energies: float32 [96, 128], P(('job', 'chain', 'pair')), parts along dimension 0, may hold values from 0.3 to 3
- pair_shift: float32 [96], P(('job', 'chain', 'pair')), parts along dimension 0, may hold values from -1.5 to -0.3
- ranks: int32 [96], P(('job', 'chain', 'pair')), parts along dimension 0, may hold values from 24 to 128
- neighbours: int32 [96, 32], P(('job', 'chain', 'pair')), parts along dimension 0, may hold values from 0 to 47, as said below
Outputs:
- final_amplitudes: bfloat16 [96, 128, 128], P(('job', 'chain', 'pair'), 'pno'), parts along dimension 0
- residual_norms: float32 [6], P('job'), parts along dimension 0
The draws below stay inside these ranges and needn't reach their ends.
There are 2 independent parts, one for each index of `job`. The reference program is written for one: setup_inputs(seed, part) draws one part's arguments, and reference() takes and returns one part's arrays. A program takes and returns all parts, laid end to end along the dimension named above; each array names one. Nothing has to cross between parts.
Inputs may be any that keep to these rules, and one draw needn't show every extreme that they name: `neighbours`: every coupled pair of pair g lies in the fragment of g (pairs k * 12 to (k + 1) * 12 - 1 for k = g // 12) or in one of the two fragments beside it.
All inputs are finite; a program needn't handle non-finite values.
Results may differ from the reference program's by a relative error of at most 0.015.
Values may be sent and summed in bfloat16 or wider, within the bound.
A program may use at most 64 MiB of HBM per device.

```python
import math
import jax
import jax.numpy as jnp
from jax import lax

R = 128
NB = 32
ITERS = 3
FRAG = 12
NPAIRS = 48


def draw_integrals(key, part):
    first, second = jax.random.split(jax.random.fold_in(key, 11))
    place = jnp.arange(NPAIRS, dtype=jnp.float32)
    scale = jnp.exp(jax.random.uniform(first, (NPAIRS,), minval=0.0, maxval=0.69)) * (1.0 + 9.0 * place / NPAIRS)
    base = jnp.clip(jax.random.normal(second, (NPAIRS, R, R)), -3.0, 3.0)
    return (0.1 * base * scale[:, None, None]).astype(jnp.bfloat16)


def draw_neighbours(key, part):
    first, second = jax.random.split(jax.random.fold_in(key, 23))
    offset = jax.random.randint(first, (NPAIRS, NB), -1, 2)
    home = jnp.arange(NPAIRS, dtype=jnp.int32) // FRAG
    target = jnp.clip(home[:, None] + offset, 0, NPAIRS // FRAG - 1)
    slot = jax.random.randint(second, (NPAIRS, NB), 0, FRAG)
    return (target * FRAG + slot).astype(jnp.int32)


def plant(entries, key, low, high):
    spot = [jax.random.randint(jax.random.fold_in(key, axis), (), 0, length) for axis, length in enumerate(entries.shape)]
    main_axis = entries.shape.index(max(entries.shape))
    next_to = spot[:main_axis] + [(spot[main_axis] + 1) % entries.shape[main_axis]] + spot[main_axis + 1:]
    return entries.at[tuple(spot)].set(low).at[tuple(next_to)].set(high)


def block_scale(rng, extent, cuts, low, high):
    def one(dim, shards_of):
        steps = jax.random.uniform(jax.random.fold_in(jax.random.fold_in(rng, 6), dim), (shards_of,), jnp.float32, low / len(cuts), high / len(cuts))
        return jnp.repeat(jnp.exp(steps), extent[dim] // shards_of).reshape((-1,) + (1,) * (len(extent) - dim - 1))

    loudness = one(*cuts[0])
    for cut in cuts[1:]:
        loudness = loudness * one(*cut)
    return loudness


def noise(rng, extent, deviation, reach, pieces=(), held_as=jnp.bfloat16):
    result = deviation * jax.random.normal(rng, extent, jnp.float32)
    if pieces:
        result = result * block_scale(rng, extent, pieces, -0.22, 0.18)
    return jnp.clip(result, -reach, reach).astype(held_as)


def setup_inputs(seed: int = 0, part: int = 0) -> dict:
    seeds = jax.random.split(jax.random.key(seed), 9)
    own_keys = jax.random.split(jax.random.fold_in(seeds[8], part), 9)
    amplitudes = noise(own_keys[0], (NPAIRS, R, R), 0.3, 4.0, ((0, 8), (1, 2)))
    integrals = draw_integrals(jax.random.fold_in(jax.random.fold_in(seeds[8], part), 71), part)
    intersections = noise(own_keys[2], (NPAIRS, NB, R, R), R ** -0.5, 0.5, ((0, 8),))
    coupling = noise(own_keys[3], (NPAIRS, NB), 1.0, 4.0, ((0, 8),), jnp.float32)
    pno_energies = jnp.clip(jnp.exp(math.log(3.0) - 2.3025851 * jax.random.uniform(own_keys[4], (NPAIRS, R), jnp.float32) ** block_scale(own_keys[4], (NPAIRS, R), ((0, 8),), -0.2, 0.2)), 0.3, 3.0)
    pair_shift = jnp.clip(-1.5 + 1.2 * jax.random.uniform(own_keys[5], (NPAIRS,), jnp.float32) ** block_scale(own_keys[5], (NPAIRS,), ((0, 8),), -0.2, 0.2), -1.5, -0.3)
    ranks = plant(jax.random.randint(own_keys[6], (NPAIRS,), 24, R + 1), jax.random.fold_in(own_keys[6], 1), 24, R).astype(jnp.int32)
    neighbours = draw_neighbours(jax.random.fold_in(jax.random.fold_in(seeds[8], part), 71), part)
    return dict(amplitudes=amplitudes, integrals=integrals, intersections=intersections, coupling=coupling, pno_energies=pno_energies, pair_shift=pair_shift, ranks=ranks, neighbours=neighbours)


def reference(amplitudes, integrals, intersections, coupling, pno_energies, pair_shift, ranks, neighbours):
    index = jnp.arange(R, dtype=jnp.int32)
    live = (index[None, :] < ranks[:, None]).astype(jnp.float32)
    mask = live[:, :, None] * live[:, None, :]
    denom = pno_energies[:, :, None] + pno_energies[:, None, :] - pair_shift[:, None, None]
    amps = (amplitudes.astype(jnp.float32) * mask).astype(jnp.bfloat16)
    ints = integrals.astype(jnp.float32)
    norms = []
    for step_no in range(ITERS):
        current = amps

        def pair_term(args):
            near, intersection, weights = args
            blocks = jnp.take(current, near, axis=0).astype(jnp.float32)
            over32 = intersection.astype(jnp.float32)
            proj = jnp.einsum('nab,nbc->nac', over32, blocks).astype(jnp.bfloat16)
            proj = lax.optimization_barrier(proj).astype(jnp.float32)
            terms = jnp.einsum('nac,nbc->nab', proj, over32)
            return jnp.einsum('n,nab->ab', weights, terms)
        coupled = lax.map(pair_term, (neighbours, intersections, coupling))
        amps32 = amps.astype(jnp.float32)
        resid = mask * (ints + coupled - denom * amps32)
        rms = jnp.sqrt(jnp.sum(resid * resid) / (NPAIRS * R * R))
        norms.append(rms)
        amps = (amps32 + resid / denom * (1.0 / (1.0 + rms))).astype(jnp.bfloat16)
    return (amps, jnp.stack(norms))
```

```python
import functools

import jax
import jax.numpy as jnp
from jax import lax
from jax.experimental import pallas as pl
from jax.experimental.pallas import tpu as pltpu
from jax.sharding import PartitionSpec as P

ITERS = 3
MESH = pl.DeviceIdType.MESH
GROUP = 4


def remote(src, dst, send_sem, recv_sem, device):
    return pltpu.make_async_remote_copy(
        src_ref=src,
        dst_ref=dst,
        send_sem=send_sem,
        recv_sem=recv_sem,
        device_id=device,
        device_id_type=MESH,
    )


def kernel(
    nchain,
    npair,
    npno,
    cells,
    nb_ref,
    coupling_ref,
    shift_ref,
    ranks_ref,
    amps_ref,
    ints_ref,
    energy_ref,
    inter_hbm,
    out_ref,
    norms_ref,
    s_vm,
    scat,
    win,
    moved,
    part,
    half_in,
    denom,
    own,
    delta,
    sums,
    load_sem,
    x_send,
    x_recv,
    p_send,
    p_recv,
    r_send,
    r_recv,
):
    z = lax.axis_index("chain")
    x = lax.axis_index("pair")
    c = lax.axis_index("pno")
    count, half, width = amps_ref.shape
    near = nb_ref.shape[1]
    total = nchain * npair * npno
    me = (z * npair + x) * npno + c
    frag = count * npair
    own_base = frag + x * count
    row0 = pl.multiple_of(c * half, half)
    row1 = pl.multiple_of((1 - c) * half, half)
    other = {"pno": 1 - c}

    loads = [pltpu.make_async_copy(inter_hbm.at[p], s_vm.at[p], load_sem.at[p]) for p in range(count)]
    for load in loads:
        load.start()

    arrive = [moved.at[t] for t in range(ITERS - 1)]
    stages = [win] + arrive

    def peer_of(j):
        peer = lax.rem(me + j, total)
        return {
            "chain": peer // (npair * npno),
            "pair": lax.rem(peer // npno, npair),
            "pno": lax.rem(peer, npno),
        }

    barrier = pltpu.get_barrier_semaphore()

    @pl.loop(1, total)
    def _(j):
        pl.semaphore_signal(barrier, inc=1, device_id=peer_of(j), device_id_type=MESH)

    rows = row0 + lax.broadcasted_iota(jnp.int32, (half, width), 0)
    cols = lax.broadcasted_iota(jnp.int32, (half, width), 1)

    def live(p):
        rank = ranks_ref[p]
        return (rows < rank) & (cols < rank)

    for p in range(count):
        mine = jnp.where(live(p), amps_ref[p].astype(jnp.float32), 0.0)
        own[p] = mine
        win[own_base + p] = mine.astype(jnp.bfloat16)

    @pl.when(z == 0)
    def _():
        for ref in stages:
            ref[pl.ds(0, frag)] = jnp.zeros((frag, half, width), jnp.bfloat16)

    @pl.when(z == nchain - 1)
    def _():
        for ref in stages:
            ref[pl.ds(2 * frag, frag)] = jnp.zeros((frag, half, width), jnp.bfloat16)

    pl.semaphore_wait(barrier, total - 1)

    partners = [
        (dz, dx) for dx in range(npair - 1, -1, -1) for dz in (-1, 1, 0) if (dz, dx) != (0, 0)
    ]

    def each_partner(act):
        for dz, dx in partners:
            if dz == 0:
                act(dz, dx)
            else:
                inside = (z > 0) if dz < 0 else (z < nchain - 1)
                pl.when(inside)(functools.partial(act, dz, dx))

    def push(t, first, size):
        def act(dz, dx):
            target = {"chain": z + dz, "pair": lax.rem(x + dx, npair)}
            dst = (1 - dz) * frag + x * count + first
            remote(
                stages[t].at[pl.ds(own_base + first, size)],
                stages[t].at[pl.ds(dst, size)],
                x_send.at[t, dz + 1, dx],
                x_recv.at[t, 1 - dz, dx],
                target,
            ).start()

        each_partner(act)

    def settle(t):
        def act(dz, dx):
            target = {"chain": z + dz, "pair": lax.rem(x + dx, npair)}
            sx = (npair - dx) % npair
            src = (1 + dz) * frag + lax.rem(x + dx, npair) * count
            copy = remote(
                stages[t].at[pl.ds(own_base, count)],
                stages[t].at[pl.ds(src, count)],
                x_send.at[t, dz + 1, dx],
                x_recv.at[t, dz + 1, sx],
                target,
            )
            copy.wait_send()
            copy.wait_recv()

        each_partner(act)

    push(0, 0, count)

    for p in range(count):
        e = energy_ref[pl.ds(p, 1), :]
        down = jnp.transpose(jnp.broadcast_to(e, (width, width)))
        part[0, p] = down
        denom[p] = part[0, p, pl.ds(row0, half), :] + e - shift_ref[p]

    for p in range(count):
        loads[p].wait()

    def pack(start):
        @pl.loop(0, count)
        def _(p):
            for k in range(near // 2):
                first = s_vm[p, 2 * k][:, start : start + half]
                second = s_vm[p, 2 * k + 1][:, start : start + half]
                scat[p, k] = jnp.concatenate([first, second], axis=1)

    for core in range(npno):
        pl.when(c == core)(functools.partial(pack, core * half))

    settle(0)
    base = (z - 1) * frag

    def partial_sum(t, p):
        acc = jnp.zeros((width, width), jnp.float32)
        for g in range(near // GROUP):
            qs = []
            for n in range(g * GROUP, (g + 1) * GROUP):
                block = win[jnp.clip(nb_ref[p, n] - base, 0, 3 * frag - 1)]
                q = lax.dot_general(
                    block,
                    s_vm[p, n],
                    (((1,), (1,)), ((), ())),
                    preferred_element_type=jnp.float32,
                )
                qs.append((q * coupling_ref[p, n]).astype(jnp.bfloat16))
            lhs = jnp.concatenate(
                [scat[p, k] for k in range(g * GROUP // 2, (g + 1) * GROUP // 2)], axis=1
            )
            acc += jnp.dot(lhs, jnp.concatenate(qs, axis=0), preferred_element_type=jnp.float32)
        part[t, p] = acc

    def swap(t, p):
        return remote(
            part.at[t, p, pl.ds(row1, half)],
            half_in.at[t, p],
            p_send.at[t, p],
            p_recv.at[t, p],
            other,
        )

    def finish(t, p, squares):
        swap(t, p).wait_recv()
        coupled = part[t, p, pl.ds(row0, half), :] + half_in[t, p]
        d = denom[p]
        resid = jnp.where(live(p), ints_ref[p].astype(jnp.float32) + coupled - d * own[p], 0.0)
        step = resid / d
        delta[p] = step
        if t + 1 < ITERS:
            arrive[t][own_base + p] = step.astype(jnp.bfloat16)
            push(t + 1, p, 1)
        return squares + jnp.sum((resid * resid).reshape(half // 8, 8, width), axis=0)

    for t in range(ITERS):
        partial_sum(t, 0)
        swap(t, 0).start()

        def body(p, squares):
            partial_sum(t, p)
            swap(t, p).start()
            return finish(t, p - 1, squares)

        squares = lax.fori_loop(1, count, body, jnp.zeros((8, width), jnp.float32))
        squares = finish(t, count - 1, squares)
        sums[t, me] = squares

        @pl.loop(1, total)
        def _(j):
            remote(sums.at[t, me], sums.at[t, me], r_send.at[t], r_recv.at[t], peer_of(j)).start()

        for p in range(count):
            swap(t, p).wait_send()
        everyone = remote(
            sums.at[t, pl.ds(0, total - 1)],
            sums.at[t, pl.ds(0, total - 1)],
            r_send.at[t],
            r_recv.at[t],
            other,
        )
        everyone.wait_send()
        everyone.wait_recv()
        squares = jnp.sum(jnp.sum(sums[t], axis=0))
        rms = jnp.sqrt(jnp.full((8, width), squares, jnp.float32) / cells)
        norms_ref[t] = rms
        factor = 1.0 / (1.0 + rms[0:1, :])
        more = t + 1 < ITERS
        for p in range(count):
            fresh = (own[p] + delta[p] * factor).astype(jnp.bfloat16)
            if more:
                own[p] = fresh.astype(jnp.float32)
            else:
                out_ref[p] = fresh
        if more:
            settle(t + 1)

            @pl.loop(0, 3 * npair)
            def _(k):
                for i in range(count):
                    at = k * count + i
                    change = arrive[t][at].astype(jnp.float32) * factor
                    win[at] = (win[at].astype(jnp.float32) + change).astype(jnp.bfloat16)


def per_device(
    amplitudes, integrals, intersections, coupling, pno_energies, pair_shift, ranks, neighbours
):
    nchain, npair, npno = (lax.axis_size(a) for a in ("chain", "pair", "pno"))
    count, half, width = amplitudes.shape
    near = neighbours.shape[1]
    frag = count * npair
    total = nchain * npair * npno
    cells = frag * nchain * width * width
    vmem = pl.BlockSpec(memory_space=pltpu.VMEM)
    smem = pl.BlockSpec(memory_space=pltpu.SMEM)
    dma = pltpu.SemaphoreType.DMA
    out, norms = pl.pallas_call(
        functools.partial(kernel, nchain, npair, npno, cells),
        out_shape=(
            jax.ShapeDtypeStruct((count, half, width), jnp.bfloat16),
            jax.ShapeDtypeStruct((ITERS, 8, width), jnp.float32),
        ),
        in_specs=[smem, smem, smem, smem, vmem, vmem, vmem, pl.BlockSpec(memory_space=pl.ANY)],
        out_specs=(vmem, vmem),
        scratch_shapes=[
            pltpu.VMEM((count, near, width, width), jnp.bfloat16),
            pltpu.VMEM((count, near // 2, width, width), jnp.bfloat16),
            pltpu.VMEM((3 * frag, half, width), jnp.bfloat16),
            pltpu.VMEM((ITERS - 1, 3 * frag, half, width), jnp.bfloat16),
            pltpu.VMEM((ITERS, count, width, width), jnp.float32),
            pltpu.VMEM((ITERS, count, half, width), jnp.float32),
            pltpu.VMEM((count, half, width), jnp.float32),
            pltpu.VMEM((count, half, width), jnp.float32),
            pltpu.VMEM((count, half, width), jnp.float32),
            pltpu.VMEM((ITERS, total, 8, width), jnp.float32),
            dma((count,)),
            dma((ITERS, 3, npair)),
            dma((ITERS, 3, npair)),
            dma((ITERS, count)),
            dma((ITERS, count)),
            dma((ITERS,)),
            dma((ITERS,)),
        ],
        compiler_params=pltpu.CompilerParams(
            collective_id=0, has_side_effects=True, vmem_limit_bytes=56 * 1024 * 1024
        ),
    )(
        neighbours,
        coupling,
        pair_shift,
        ranks,
        amplitudes,
        integrals,
        pno_energies,
        intersections,
    )
    return out, norms[:, 0, 0]


def solution(mesh):
    lead = ("job", "chain", "pair")
    in_specs = (
        P(lead, "pno", None),
        P(lead, "pno", None),
        P(lead, None, None, None),
        P(lead, None),
        P(lead, None),
        P(lead),
        P(lead),
        P(lead, None),
    )
    out_specs = (P(lead, "pno", None), P("job"))
    return jax.shard_map(
        per_device, mesh=mesh, in_specs=in_specs, out_specs=out_specs, check_vma=False
    )
```

```python
import functools

import jax
import jax.numpy as jnp
from jax import lax
from jax.experimental import pallas as pl
from jax.experimental.pallas import tpu as pltpu
from jax.sharding import PartitionSpec as P

ITERS = 3
MESH = pl.DeviceIdType.MESH
GROUP = 4


def remote(src, dst, send_sem, recv_sem, device):
    return pltpu.make_async_remote_copy(
        src_ref=src,
        dst_ref=dst,
        send_sem=send_sem,
        recv_sem=recv_sem,
        device_id=device,
        device_id_type=MESH,
    )


def kernel(
    nchain,
    npair,
    npno,
    cells,
    nb_ref,
    coupling_ref,
    shift_ref,
    ranks_ref,
    amps_ref,
    ints_ref,
    energy_ref,
    inter_hbm,
    out_ref,
    norms_ref,
    s_vm,
    scat,
    stages,
    part,
    half_in,
    denom,
    own,
    delta,
    csum,
    factor,
    sums,
    load_sem,
    x_send,
    x_recv,
    p_send,
    p_recv,
    r_send,
    r_recv,
):
    z = lax.axis_index("chain")
    x = lax.axis_index("pair")
    c = lax.axis_index("pno")
    count, half, width = amps_ref.shape
    near = nb_ref.shape[1]
    total = nchain * npair * npno
    me = (z * npair + x) * npno + c
    frag = count * npair
    own_base = frag + x * count
    row0 = pl.multiple_of(c * half, half)
    row1 = pl.multiple_of((1 - c) * half, half)
    other = {"pno": 1 - c}

    loads = [pltpu.make_async_copy(inter_hbm.at[p], s_vm.at[p], load_sem.at[p]) for p in range(count)]
    for load in loads:
        load.start()

    win, arrive = stages[0], stages[1:]

    def peer_of(j):
        peer = lax.rem(me + j, total)
        return {
            "chain": peer // (npair * npno),
            "pair": lax.rem(peer // npno, npair),
            "pno": lax.rem(peer, npno),
        }

    barrier = pltpu.get_barrier_semaphore()

    @pl.loop(1, total)
    def _(j):
        pl.semaphore_signal(barrier, inc=1, device_id=peer_of(j), device_id_type=MESH)

    rows = row0 + lax.broadcasted_iota(jnp.int32, (half, width), 0)
    cols = lax.broadcasted_iota(jnp.int32, (half, width), 1)

    def live(p):
        rank = ranks_ref[p]
        return (rows < rank) & (cols < rank)

    for p in range(count):
        mine = jnp.where(live(p), amps_ref[p].astype(jnp.float32), 0.0)
        own[p] = mine
        win[own_base + p] = mine.astype(jnp.bfloat16)

    @pl.when(z == 0)
    def _():
        for ref in stages:
            ref[pl.ds(0, frag)] = jnp.zeros((frag, half, width), jnp.bfloat16)

    @pl.when(z == nchain - 1)
    def _():
        for ref in stages:
            ref[pl.ds(2 * frag, frag)] = jnp.zeros((frag, half, width), jnp.bfloat16)

    pl.semaphore_wait(barrier, total - 1)

    partners = [
        (dz, dx) for dx in range(npair - 1, -1, -1) for dz in (-1, 1, 0) if (dz, dx) != (0, 0)
    ]

    def each_partner(act):
        for dz, dx in partners:
            if dz == 0:
                act(dz, dx)
            else:
                inside = (z > 0) if dz < 0 else (z < nchain - 1)
                pl.when(inside)(functools.partial(act, dz, dx))

    def push(t, first, size):
        def act(dz, dx):
            target = {"chain": z + dz, "pair": lax.rem(x + dx, npair)}
            dst = (1 - dz) * frag + x * count + first
            remote(
                stages[t].at[pl.ds(own_base + first, size)],
                stages[t].at[pl.ds(dst, size)],
                x_send.at[t, dz + 1, dx],
                x_recv.at[t, 1 - dz, dx],
                target,
            ).start()

        each_partner(act)

    def settle(t):
        def act(dz, dx):
            target = {"chain": z + dz, "pair": lax.rem(x + dx, npair)}
            sx = (npair - dx) % npair
            src = (1 + dz) * frag + lax.rem(x + dx, npair) * count
            copy = remote(
                stages[t].at[pl.ds(own_base, count)],
                stages[t].at[pl.ds(src, count)],
                x_send.at[t, dz + 1, dx],
                x_recv.at[t, dz + 1, sx],
                target,
            )
            copy.wait_send()
            copy.wait_recv()

        each_partner(act)

    push(0, 0, count)

    for p in range(count):
        e = energy_ref[pl.ds(p, 1), :]
        down = jnp.transpose(jnp.broadcast_to(e, (width, width)))
        part[0, p] = down
        denom[p] = part[0, p, pl.ds(row0, half), :] + e - shift_ref[p]

    for p in range(count):
        loads[p].wait()

    def pack(start):
        @pl.loop(0, count)
        def _(p):
            for k in range(near // 2):
                first = s_vm[p, 2 * k][:, start : start + half]
                second = s_vm[p, 2 * k + 1][:, start : start + half]
                scat[p, k] = jnp.concatenate([first, second], axis=1)

    for core in range(npno):
        pl.when(c == core)(functools.partial(pack, core * half))

    settle(0)
    base = (z - 1) * frag

    def partial_sum(t, p):
        source = stages[t]
        acc = jnp.zeros((width, width), jnp.float32)
        for g in range(near // GROUP):
            qs = []
            for n in range(g * GROUP, (g + 1) * GROUP):
                block = source[jnp.clip(nb_ref[p, n] - base, 0, 3 * frag - 1)]
                q = lax.dot_general(
                    block,
                    s_vm[p, n],
                    (((1,), (1,)), ((), ())),
                    preferred_element_type=jnp.float32,
                )
                qs.append((q * coupling_ref[p, n]).astype(jnp.bfloat16))
            lhs = jnp.concatenate(
                [scat[p, k] for k in range(g * GROUP // 2, (g + 1) * GROUP // 2)], axis=1
            )
            acc += jnp.dot(lhs, jnp.concatenate(qs, axis=0), preferred_element_type=jnp.float32)
        part[t, p] = acc

    def swap(t, p):
        return remote(
            part.at[t, p, pl.ds(row1, half)],
            half_in.at[t, p],
            p_send.at[t, p],
            p_recv.at[t, p],
            other,
        )

    def finish(t, p, squares):
        swap(t, p).wait_recv()
        coupled = part[t, p, pl.ds(row0, half), :] + half_in[t, p]
        mine = own[p]
        if t > 0:
            coupled = csum[p] + factor[0:1, :] * coupled
            mine = (mine + delta[p] * factor[0:1, :]).astype(jnp.bfloat16).astype(jnp.float32)
            own[p] = mine
        csum[p] = coupled
        d = denom[p]
        resid = jnp.where(live(p), ints_ref[p].astype(jnp.float32) + coupled - d * mine, 0.0)
        step = resid / d
        delta[p] = step
        if t + 1 < ITERS:
            arrive[t][own_base + p] = step.astype(jnp.bfloat16)
            push(t + 1, p, 1)
        return squares + jnp.sum((resid * resid).reshape(half // 8, 8, width), axis=0)

    def absorb(t):
        everyone = remote(
            sums.at[t, pl.ds(0, total - 1)],
            sums.at[t, pl.ds(0, total - 1)],
            r_send.at[t],
            r_recv.at[t],
            other,
        )
        everyone.wait_send()
        everyone.wait_recv()
        squares = jnp.sum(jnp.sum(sums[t], axis=0))
        rms = jnp.sqrt(jnp.full((8, width), squares, jnp.float32) / cells)
        norms_ref[t] = rms
        factor[...] = 1.0 / (1.0 + rms)

    for t in range(ITERS):
        partial_sum(t, 0)
        swap(t, 0).start()

        def body(p, squares):
            partial_sum(t, p)
            swap(t, p).start()
            if t > 0:
                pl.when(p == 1)(functools.partial(absorb, t - 1))
            return finish(t, p - 1, squares)

        squares = lax.fori_loop(1, count, body, jnp.zeros((8, width), jnp.float32))
        squares = finish(t, count - 1, squares)
        sums[t, me] = squares

        @pl.loop(1, total)
        def _(j):
            remote(sums.at[t, me], sums.at[t, me], r_send.at[t], r_recv.at[t], peer_of(j)).start()

        for p in range(count):
            swap(t, p).wait_send()
        if t + 1 < ITERS:
            settle(t + 1)

    absorb(ITERS - 1)
    for p in range(count):
        out_ref[p] = (own[p] + delta[p] * factor[0:1, :]).astype(jnp.bfloat16)


def per_device(
    amplitudes, integrals, intersections, coupling, pno_energies, pair_shift, ranks, neighbours
):
    nchain, npair, npno = (lax.axis_size(a) for a in ("chain", "pair", "pno"))
    count, half, width = amplitudes.shape
    near = neighbours.shape[1]
    frag = count * npair
    total = nchain * npair * npno
    cells = frag * nchain * width * width
    vmem = pl.BlockSpec(memory_space=pltpu.VMEM)
    smem = pl.BlockSpec(memory_space=pltpu.SMEM)
    dma = pltpu.SemaphoreType.DMA
    out, norms = pl.pallas_call(
        functools.partial(kernel, nchain, npair, npno, cells),
        out_shape=(
            jax.ShapeDtypeStruct((count, half, width), jnp.bfloat16),
            jax.ShapeDtypeStruct((ITERS, 8, width), jnp.float32),
        ),
        in_specs=[smem, smem, smem, smem, vmem, vmem, vmem, pl.BlockSpec(memory_space=pl.ANY)],
        out_specs=(vmem, vmem),
        scratch_shapes=[
            pltpu.VMEM((count, near, width, width), jnp.bfloat16),
            pltpu.VMEM((count, near // 2, width, width), jnp.bfloat16),
            [pltpu.VMEM((3 * frag, half, width), jnp.bfloat16) for _ in range(ITERS)],
            pltpu.VMEM((ITERS, count, width, width), jnp.float32),
            pltpu.VMEM((ITERS, count, half, width), jnp.float32),
            pltpu.VMEM((count, half, width), jnp.float32),
            pltpu.VMEM((count, half, width), jnp.float32),
            pltpu.VMEM((count, half, width), jnp.float32),
            pltpu.VMEM((count, half, width), jnp.float32),
            pltpu.VMEM((8, width), jnp.float32),
            pltpu.VMEM((ITERS, total, 8, width), jnp.float32),
            dma((count,)),
            dma((ITERS, 3, npair)),
            dma((ITERS, 3, npair)),
            dma((ITERS, count)),
            dma((ITERS, count)),
            dma((ITERS,)),
            dma((ITERS,)),
        ],
        compiler_params=pltpu.CompilerParams(
            collective_id=0, has_side_effects=True, vmem_limit_bytes=56 * 1024 * 1024
        ),
    )(
        neighbours,
        coupling,
        pair_shift,
        ranks,
        amplitudes,
        integrals,
        pno_energies,
        intersections,
    )
    return out, norms[:, 0, 0]


def solution(mesh):
    lead = ("job", "chain", "pair")
    in_specs = (
        P(lead, "pno", None),
        P(lead, "pno", None),
        P(lead, None, None, None),
        P(lead, None),
        P(lead, None),
        P(lead),
        P(lead),
        P(lead, None),
    )
    out_specs = (P(lead, "pno", None), P("job"))
    return jax.shard_map(
        per_device, mesh=mesh, in_specs=in_specs, out_specs=out_specs, check_vma=False
    )
```

```python
import functools

import jax
import jax.numpy as jnp
from jax import lax
from jax.experimental import pallas as pl
from jax.experimental.pallas import tpu as pltpu
from jax.sharding import PartitionSpec as P

ITERS = 3
MESH = pl.DeviceIdType.MESH
GROUP = 16


def remote(src, dst, send_sem, recv_sem, device):
    return pltpu.make_async_remote_copy(
        src_ref=src,
        dst_ref=dst,
        send_sem=send_sem,
        recv_sem=recv_sem,
        device_id=device,
        device_id_type=MESH,
    )


def kernel(
    nchain,
    npair,
    npno,
    cells,
    nb_ref,
    coupling_ref,
    shift_ref,
    ranks_ref,
    amps_ref,
    ints_ref,
    energy_ref,
    inter_hbm,
    out_ref,
    norms_ref,
    s_vm,
    scat,
    stages,
    part,
    half_in,
    denom,
    own,
    delta,
    csum,
    factor,
    sums,
    load_sem,
    x_send,
    x_recv,
    p_send,
    p_recv,
    r_send,
    r_recv,
):
    z = lax.axis_index("chain")
    x = lax.axis_index("pair")
    c = lax.axis_index("pno")
    count, half, width = amps_ref.shape
    near = nb_ref.shape[1]
    total = nchain * npair * npno
    me = (z * npair + x) * npno + c
    frag = count * npair
    own_base = frag + x * count
    row0 = pl.multiple_of(c * half, half)
    row1 = pl.multiple_of((1 - c) * half, half)
    other = {"pno": 1 - c}

    loads = [pltpu.make_async_copy(inter_hbm.at[p], s_vm.at[p], load_sem.at[p]) for p in range(count)]
    for load in loads:
        load.start()

    win, arrive = stages[0], stages[1:]

    def peer_of(j):
        peer = lax.rem(me + j, total)
        return {
            "chain": peer // (npair * npno),
            "pair": lax.rem(peer // npno, npair),
            "pno": lax.rem(peer, npno),
        }

    barrier = pltpu.get_barrier_semaphore()

    @pl.loop(1, total)
    def _(j):
        pl.semaphore_signal(barrier, inc=1, device_id=peer_of(j), device_id_type=MESH)

    rows = row0 + lax.broadcasted_iota(jnp.int32, (half, width), 0)
    cols = lax.broadcasted_iota(jnp.int32, (half, width), 1)

    def live(p):
        rank = ranks_ref[p]
        return (rows < rank) & (cols < rank)

    for p in range(count):
        mine = jnp.where(live(p), amps_ref[p].astype(jnp.float32), 0.0)
        own[p] = mine
        win[own_base + p] = mine.astype(jnp.bfloat16)

    @pl.when(z == 0)
    def _():
        for ref in stages:
            ref[pl.ds(0, frag)] = jnp.zeros((frag, half, width), jnp.bfloat16)

    @pl.when(z == nchain - 1)
    def _():
        for ref in stages:
            ref[pl.ds(2 * frag, frag)] = jnp.zeros((frag, half, width), jnp.bfloat16)

    pl.semaphore_wait(barrier, total - 1)

    partners = [
        (dz, dx) for dx in range(npair - 1, -1, -1) for dz in (-1, 1, 0) if (dz, dx) != (0, 0)
    ]

    def each_partner(act):
        for dz, dx in partners:
            if dz == 0:
                act(dz, dx)
            else:
                inside = (z > 0) if dz < 0 else (z < nchain - 1)
                pl.when(inside)(functools.partial(act, dz, dx))

    def push(t, first, size):
        def act(dz, dx):
            target = {"chain": z + dz, "pair": lax.rem(x + dx, npair)}
            dst = (1 - dz) * frag + x * count + first
            remote(
                stages[t].at[pl.ds(own_base + first, size)],
                stages[t].at[pl.ds(dst, size)],
                x_send.at[t, dz + 1, dx],
                x_recv.at[t, 1 - dz, dx],
                target,
            ).start()

        each_partner(act)

    def settle(t):
        def act(dz, dx):
            target = {"chain": z + dz, "pair": lax.rem(x + dx, npair)}
            sx = (npair - dx) % npair
            src = (1 + dz) * frag + lax.rem(x + dx, npair) * count
            copy = remote(
                stages[t].at[pl.ds(own_base, count)],
                stages[t].at[pl.ds(src, count)],
                x_send.at[t, dz + 1, dx],
                x_recv.at[t, dz + 1, sx],
                target,
            )
            copy.wait_send()
            copy.wait_recv()

        each_partner(act)

    push(0, 0, count)

    for p in range(count):
        e = energy_ref[pl.ds(p, 1), :]
        down = jnp.transpose(jnp.broadcast_to(e, (width, width)))
        part[0, p] = down
        denom[p] = part[0, p, pl.ds(row0, half), :] + e - shift_ref[p]

    for p in range(count):
        loads[p].wait()

    def pack(start):
        @pl.loop(0, count)
        def _(p):
            for k in range(near // 2):
                first = s_vm[p, 2 * k][:, start : start + half]
                second = s_vm[p, 2 * k + 1][:, start : start + half]
                scat[p, k] = jnp.concatenate([first, second], axis=1)

    for core in range(npno):
        pl.when(c == core)(functools.partial(pack, core * half))

    settle(0)
    base = (z - 1) * frag

    def partial_sum(t, p):
        source = stages[t]
        acc = jnp.zeros((width, width), jnp.float32)
        for g in range(near // GROUP):
            qs = []
            for n in range(g * GROUP, (g + 1) * GROUP):
                block = source[jnp.clip(nb_ref[p, n] - base, 0, 3 * frag - 1)]
                q = lax.dot_general(
                    block,
                    s_vm[p, n],
                    (((1,), (1,)), ((), ())),
                    preferred_element_type=jnp.float32,
                )
                qs.append((q * coupling_ref[p, n]).astype(jnp.bfloat16))
            lhs = jnp.concatenate(
                [scat[p, k] for k in range(g * GROUP // 2, (g + 1) * GROUP // 2)], axis=1
            )
            acc += jnp.dot(lhs, jnp.concatenate(qs, axis=0), preferred_element_type=jnp.float32)
        part[t, p] = acc

    def swap(t, p):
        return remote(
            part.at[t, p, pl.ds(row1, half)],
            half_in.at[t, p],
            p_send.at[t, p],
            p_recv.at[t, p],
            other,
        )

    def finish(t, p, squares):
        swap(t, p).wait_recv()
        coupled = part[t, p, pl.ds(row0, half), :] + half_in[t, p]
        mine = own[p]
        if t > 0:
            coupled = csum[p] + factor[0:1, :] * coupled
            mine = (mine + delta[p] * factor[0:1, :]).astype(jnp.bfloat16).astype(jnp.float32)
            own[p] = mine
        csum[p] = coupled
        d = denom[p]
        resid = jnp.where(live(p), ints_ref[p].astype(jnp.float32) + coupled - d * mine, 0.0)
        step = resid / d
        delta[p] = step
        if t + 1 < ITERS:
            arrive[t][own_base + p] = step.astype(jnp.bfloat16)
            push(t + 1, p, 1)
        return squares + jnp.sum((resid * resid).reshape(half // 8, 8, width), axis=0)

    def absorb(t):
        everyone = remote(
            sums.at[t, pl.ds(0, total - 1)],
            sums.at[t, pl.ds(0, total - 1)],
            r_send.at[t],
            r_recv.at[t],
            other,
        )
        everyone.wait_send()
        everyone.wait_recv()
        squares = jnp.sum(jnp.sum(sums[t], axis=0))
        rms = jnp.sqrt(jnp.full((8, width), squares, jnp.float32) / cells)
        norms_ref[t] = rms
        factor[...] = 1.0 / (1.0 + rms)

    for t in range(ITERS):
        partial_sum(t, 0)
        swap(t, 0).start()

        def body(p, squares):
            partial_sum(t, p)
            swap(t, p).start()
            if t > 0:
                pl.when(p == 1)(functools.partial(absorb, t - 1))
            return finish(t, p - 1, squares)

        squares = lax.fori_loop(1, count, body, jnp.zeros((8, width), jnp.float32))
        squares = finish(t, count - 1, squares)
        sums[t, me] = squares

        @pl.loop(1, total)
        def _(j):
            remote(sums.at[t, me], sums.at[t, me], r_send.at[t], r_recv.at[t], peer_of(j)).start()

        for p in range(count):
            swap(t, p).wait_send()
        if t + 1 < ITERS:
            settle(t + 1)

    absorb(ITERS - 1)
    for p in range(count):
        out_ref[p] = (own[p] + delta[p] * factor[0:1, :]).astype(jnp.bfloat16)


def per_device(
    amplitudes, integrals, intersections, coupling, pno_energies, pair_shift, ranks, neighbours
):
    nchain, npair, npno = (lax.axis_size(a) for a in ("chain", "pair", "pno"))
    count, half, width = amplitudes.shape
    near = neighbours.shape[1]
    frag = count * npair
    total = nchain * npair * npno
    cells = frag * nchain * width * width
    vmem = pl.BlockSpec(memory_space=pltpu.VMEM)
    smem = pl.BlockSpec(memory_space=pltpu.SMEM)
    dma = pltpu.SemaphoreType.DMA
    out, norms = pl.pallas_call(
        functools.partial(kernel, nchain, npair, npno, cells),
        out_shape=(
            jax.ShapeDtypeStruct((count, half, width), jnp.bfloat16),
            jax.ShapeDtypeStruct((ITERS, 8, width), jnp.float32),
        ),
        in_specs=[smem, smem, smem, smem, vmem, vmem, vmem, pl.BlockSpec(memory_space=pl.ANY)],
        out_specs=(vmem, vmem),
        scratch_shapes=[
            pltpu.VMEM((count, near, width, width), jnp.bfloat16),
            pltpu.VMEM((count, near // 2, width, width), jnp.bfloat16),
            [pltpu.VMEM((3 * frag, half, width), jnp.bfloat16) for _ in range(ITERS)],
            pltpu.VMEM((ITERS, count, width, width), jnp.float32),
            pltpu.VMEM((ITERS, count, half, width), jnp.float32),
            pltpu.VMEM((count, half, width), jnp.float32),
            pltpu.VMEM((count, half, width), jnp.float32),
            pltpu.VMEM((count, half, width), jnp.float32),
            pltpu.VMEM((count, half, width), jnp.float32),
            pltpu.VMEM((8, width), jnp.float32),
            pltpu.VMEM((ITERS, total, 8, width), jnp.float32),
            dma((count,)),
            dma((ITERS, 3, npair)),
            dma((ITERS, 3, npair)),
            dma((ITERS, count)),
            dma((ITERS, count)),
            dma((ITERS,)),
            dma((ITERS,)),
        ],
        compiler_params=pltpu.CompilerParams(
            collective_id=0, has_side_effects=True, vmem_limit_bytes=56 * 1024 * 1024
        ),
    )(
        neighbours,
        coupling,
        pair_shift,
        ranks,
        amplitudes,
        integrals,
        pno_energies,
        intersections,
    )
    return out, norms[:, 0, 0]


def solution(mesh):
    lead = ("job", "chain", "pair")
    in_specs = (
        P(lead, "pno", None),
        P(lead, "pno", None),
        P(lead, None, None, None),
        P(lead, None),
        P(lead, None),
        P(lead),
        P(lead),
        P(lead, None),
    )
    out_specs = (P(lead, "pno", None), P("job"))
    return jax.shard_map(
        per_device, mesh=mesh, in_specs=in_specs, out_specs=out_specs, check_vma=False
    )
```
